32 devices in a mesh: grp: 4 (over y, x), dev: 8 (over z, core).
Axes of the slice: x: 2, y: 2, z: 4, core: 2. Of those that a mesh axis runs over, the one named last changes fastest.
Arguments:
- q_lat: bfloat16 [128, 64, 576], P(('grp', 'dev')), parts along dimension 0, may hold values from -40 to 40
- latent_cache: bfloat16 [128, 256, 576], P(('grp', 'dev')), parts along dimension 0, may hold values from -8 to 8
- lengths: int32 [128], P('grp'), parts along dimension 0, may hold values from 32 to 256, as said below
- moves: int32 [64, 3], P('grp'), parts along dimension 0, may hold values from 0 to 31, as said below
- hidden_in: bfloat16 [128, 3584], P(('grp', 'dev')), parts along dimension 0, may hold values from -6 to 6
- norm_gain: bfloat16 [3584], replicated, may hold values from 0.25 to 1.75
- w_up: bfloat16 [3584, 10240], P(None, 'dev'), may hold values from -0.09375 to 0.09375
- w_down: bfloat16 [10240, 3584], P('dev'), may hold values from -0.0625 to 0.0625
- queue_counts: int32 [32, 8], P(('grp', 'dev')), parts along dimension 0, may hold values from 0 to 63
- deadline: int32 [128], P(('grp', 'dev')), parts along dimension 0, may hold values from 0 to 7
Outputs:
- attn_out: bfloat16 [128, 64, 512], P(('grp', 'dev')), parts along dimension 0
- new_cache: bfloat16 [128, 256, 576], P(('grp', 'dev')), parts along dimension 0
- mixed: bfloat16 [128, 3584], P(('grp', 'dev')), parts along dimension 0
- bucket_load: float32 [32], P('grp'), parts along dimension 0
The draws below stay inside these ranges and needn't reach their ends.
There are 4 independent parts, one for each index of `grp`. The reference program is written for one: setup_inputs(seed, part) draws one part's arguments, and reference() takes and returns one part's arrays. A program takes and returns all parts, laid end to end along the dimension named above; an argument that names none is the same for every part. Nothing has to cross between parts.
Inputs may be any that keep to these rules, and one draw needn't show every extreme that they name: `lengths`: every length is at least 32; some request has exactly 256. `moves`: entry j * 8 + s (j below 2) has source device s and names a request of device s (requests r lie on device r // 4); the requests listed for one device are distinct. In round j every source s sends to (s + k_j) mod 8, with k_j between 1 and 7 the same for all sources of the round and different between rounds; one of the rounds has k_j = 4.
All inputs are finite; a program needn't handle non-finite values.
Results may differ from the reference program's by a relative error of at most 0.002.
The reference program's roundings to bfloat16 on the way count: a program that leaves them out, or rounds other values in their place, can miss the bound.
Values may be sent and summed in bfloat16 or wider, within the bound.
A program may use at most 128 MiB of HBM per device.

```python
import jax
import jax.numpy as jnp
from jax import lax

D = 3584
FF = 10240
H = 64
KV = 576
VL = 512
CTX = 256
ROWS_DEV = 4
MOVE_DEV = 2
BUCKETS = 8
ROWS = 32
MOVES = 16
N_DEV = 8


def latent_pair(key):
    base_key = jax.random.fold_in(key, 7)
    key_cache, key_query = jax.random.split(base_key, 2)
    latent = jnp.clip(jax.random.normal(key_cache, (ROWS, CTX, KV), jnp.float32), -6.0, 6.0)
    queries = jnp.clip(jax.random.normal(key_query, (ROWS, H, KV), jnp.float32), -6.0, 6.0)
    return (queries, latent)


def draw_q_lat(key, part):
    return latent_pair(key)[0].astype(jnp.bfloat16)


def draw_latent_cache(key, part):
    return latent_pair(key)[1].astype(jnp.bfloat16)


def draw_lengths(key, part):
    key_level, key_spread, key_pick = jax.random.split(jax.random.fold_in(key, 21), 3)
    groups = ROWS // ROWS_DEV
    level = jax.random.randint(key_level, (groups,), 1, 5)
    ceiling = jnp.repeat(CTX * level // 4, ROWS_DEV)
    lowest = CTX // 8
    spread = jax.random.randint(key_spread, (ROWS,), 0, 1 << 20)
    values = lowest + spread % (ceiling - lowest + 1)
    chosen = jax.random.randint(key_pick, (), 0, ROWS)
    values = jnp.where(jnp.arange(ROWS) == chosen, CTX, values)
    return values.astype(jnp.int32)


def draw_moves(key, part):
    key_offset, key_rows, key_place = jax.random.split(jax.random.fold_in(key, 31), 3)
    groups = ROWS // ROWS_DEV
    half = groups // 2
    others = jax.random.permutation(key_offset, max(groups - 2, 1))[:MOVE_DEV - 1] + 1
    others = others + (others >= half).astype(others.dtype)
    listed = jnp.concatenate([jnp.full((1,), half, others.dtype), others])
    place = jax.random.randint(key_place, (), 0, MOVE_DEV)
    offsets = jnp.roll(listed, place)
    row_keys = jax.random.split(key_rows, groups)
    picked = jax.vmap(lambda single: jax.random.permutation(single, ROWS_DEV)[:MOVE_DEV])(row_keys)
    sources = jnp.arange(groups)
    requests = sources[None, :] * ROWS_DEV + picked.T
    targets = (sources[None, :] + offsets[:, None]) % groups
    senders = jnp.broadcast_to(sources[None, :], (MOVE_DEV, groups))
    return jnp.stack([requests, senders, targets], axis=-1).reshape(MOVES, 3).astype(jnp.int32)


def with_ends(values, own_key, least, high):
    longest = values.shape.index(max(values.shape))
    spots = []
    for shift in (0, 1):
        where = [jax.random.randint(jax.random.fold_in(own_key, axis), (), 0, length) for axis, length in enumerate(values.shape)]
        where[longest] = (where[longest] + shift) % values.shape[longest]
        spots.append(tuple(where))
    return values.at[spots[0]].set(least).at[spots[1]].set(high)


def steps_of(stream_key, extent, pieces, least, top_value):
    level = 1.0
    for axis_at, blocks in pieces:
        draws = jax.random.uniform(jax.random.fold_in(jax.random.fold_in(stream_key, 6), axis_at), (blocks,), jnp.float32, least / len(pieces), top_value / len(pieces))
        level = level * jnp.repeat(jnp.exp(draws), extent[axis_at] // blocks).reshape((-1,) + (1,) * (len(extent) - 1 - axis_at))
    return level


def scatter_about(rng, dims, scale, most, cuts=(), held_as=jnp.bfloat16):
    entries = scale * jax.random.normal(rng, dims, jnp.float32)
    if cuts:
        entries = entries * steps_of(rng, dims, cuts, -0.22, 0.18)
    return jnp.clip(entries, -most, most).astype(held_as)


def setup_inputs(seed: int = 0, part: int = 0) -> dict:
    key_of = jax.random.split(jax.random.key(seed), 11)
    own_keys = jax.random.split(jax.random.fold_in(key_of[10], part), 11)
    return {
        "q_lat": draw_q_lat(jax.random.fold_in(jax.random.fold_in(key_of[10], part), 71), part),
        "latent_cache": draw_latent_cache(jax.random.fold_in(jax.random.fold_in(key_of[10], part), 71), part),
        "lengths": draw_lengths(jax.random.fold_in(jax.random.fold_in(key_of[10], part), 71), part),
        "moves": draw_moves(jax.random.fold_in(jax.random.fold_in(key_of[10], part), 71), part),
        "hidden_in": scatter_about(own_keys[4], (ROWS, D), 1.0, 6.0, ((0, 8),)),
        "norm_gain": jnp.clip(1.0 + 0.15 * jax.random.normal(key_of[5], (D,), jnp.float32), 0.25, 1.75).astype(jnp.bfloat16),
        "w_up": scatter_about(key_of[6], (D, FF), D ** -0.5, 0.09375, ((1, 8),)),
        "w_down": scatter_about(key_of[7], (FF, D), FF ** -0.5, 0.0625, ((0, 8),)),
        "queue_counts": with_ends(jax.random.randint(own_keys[8], (N_DEV, BUCKETS), 0, 64), jax.random.fold_in(own_keys[8], 1), 0, 63).astype(jnp.int32),
        "deadline": with_ends(jax.random.randint(own_keys[9], (ROWS,), 0, BUCKETS), jax.random.fold_in(own_keys[9], 1), 0, BUCKETS - 1).astype(jnp.int32),
    }


softmax_scale = 192.0 ** (-0.5)

def attention(queries, latent, context_lengths):
    query_wide = queries.astype(jnp.float32)
    latent_wide = latent.astype(jnp.float32)
    scores = jnp.einsum('rhc,rkc->rhk', query_wide, latent_wide) * softmax_scale
    included = jnp.arange(CTX, dtype=jnp.int32)[None, None, :] < context_lengths[:, None, None]
    scores = jnp.where(included, scores, jnp.float32(-1e+30))
    largest = lax.optimization_barrier(jnp.max(scores, axis=-1, keepdims=True))
    weights = jnp.where(included, jnp.exp(scores - largest), jnp.float32(0.0))
    total = lax.optimization_barrier(jnp.sum(weights, axis=-1))
    rounded = lax.optimization_barrier(weights.astype(jnp.bfloat16))
    summed = jnp.einsum('rhk,rkc->rhc', rounded.astype(jnp.float32), latent_wide[:, :, :VL])
    return (summed / total[:, :, None]).astype(jnp.bfloat16)

def reference(q_lat, latent_cache, lengths, moves, hidden_in, norm_gain, w_up, w_down, queue_counts, deadline):
    attn_out = attention(q_lat, latent_cache, lengths)
    rounds = moves.reshape(MOVE_DEV, N_DEV, 3)
    source_rows = rounds[:, :, 0]
    target_rows = jnp.take_along_axis(source_rows, rounds[:, :, 2], axis=1)
    new_cache = latent_cache.at[target_rows.reshape(-1)].set(latent_cache[source_rows.reshape(-1)])
    widened = hidden_in.astype(jnp.float32)
    scaled = lax.rsqrt(lax.optimization_barrier(jnp.mean(widened * widened, axis=-1, keepdims=True)) + 1e-06)
    normed = (widened * scaled * norm_gain.astype(jnp.float32)[None, :]).astype(jnp.bfloat16)
    upward = jnp.dot(normed, w_up, preferred_element_type=jnp.float32)
    hidden = jax.nn.silu(upward).astype(jnp.bfloat16)
    downward = jnp.dot(hidden, w_down, preferred_element_type=jnp.float32)
    mixed = (widened + downward).astype(jnp.bfloat16)
    running = (deadline[:, None] == jnp.arange(BUCKETS, dtype=jnp.int32)[None, :]).astype(jnp.float32)
    bucket_load = lax.optimization_barrier(jnp.sum(queue_counts.astype(jnp.float32), axis=0)) + lax.optimization_barrier(jnp.sum(running, axis=0))
    return (attn_out, new_cache, mixed, bucket_load)
```

```python
import functools

import jax
import jax.numpy as jnp
from jax import lax
from jax.experimental import pallas as pl
from jax.experimental.pallas import tpu as pltpu
from jax.sharding import PartitionSpec as P

VL = 512
MOVE_DEV = 2
BUCKETS = 8
CORES = 2
MESH = pl.DeviceIdType.MESH

softmax_scale = 192.0 ** (-0.5)


def body(
    n,
    q_hbm, cache_hbm, len_ref, hid_ref, gain_ref, wu_hbm, wd_hbm, qc_ref, dl_ref, pay_hbm,
    attn_ref, arr_hbm, mixed_ref, load_ref,
    q_v, cache_v, wu_v, wd_v, allr, xs, x_v, hidden_v, part, rx1, red, rx2, loads,
    sem_in, sem_wu, sem_wd, ag_s, ag_r, fw_s, pay_s, pay_r, s1, r1, s2, r2, l_s, l_r,
):
    me = lax.axis_index("dev")
    chips = n // CORES
    z, c = me // CORES, me % CORES
    partner = z * CORES + (1 - c)
    rows, dim = hid_ref.shape
    nu, nd = wu_v.shape[0], wd_v.shape[0]
    cu, cd = wu_v.shape[2], wd_v.shape[2]
    half_rows = chips * rows

    def remote(src, dst, ss, rs, dev):
        return pltpu.make_async_remote_copy(
            src_ref=src, dst_ref=dst, send_sem=ss, recv_sem=rs,
            device_id={"dev": dev}, device_id_type=MESH)

    def up_copy(i):
        return pltpu.make_async_copy(
            wu_hbm.at[:, pl.ds(pl.multiple_of(i * cu, 128), cu)], wu_v.at[i], sem_wu.at[i])

    def down_copy(i):
        return pltpu.make_async_copy(
            wd_hbm.at[:, pl.ds(pl.multiple_of(i * cd, 128), cd)], wd_v.at[i], sem_wd.at[i])

    barrier = pltpu.get_barrier_semaphore()
    for o in range(1, n):
        pl.semaphore_signal(barrier, inc=1, device_id={"dev": lax.rem(me + o, n)},
                            device_id_type=MESH)
    q_copy = pltpu.make_async_copy(q_hbm, q_v, sem_in.at[0])
    cache_copy = pltpu.make_async_copy(cache_hbm, cache_v, sem_in.at[1])
    q_copy.start()
    cache_copy.start()
    for i in range(nu):
        up_copy(i).start()
    for i in range(nd):
        down_copy(i).start()

    widened = hid_ref[...].astype(jnp.float32)
    scaled = lax.rsqrt(jnp.mean(widened * widened, axis=-1, keepdims=True) + 1e-06)
    normed = widened * scaled * gain_ref[...].astype(jnp.float32)
    allr[me] = normed.astype(jnp.bfloat16)
    buckets = lax.broadcasted_iota(jnp.int32, (1, 128), 1)
    counted = qc_ref[...].astype(jnp.float32)
    for r in range(rows):
        counted = counted + jnp.where(buckets == dl_ref[r], 1.0, 0.0)
    loads[me] = counted
    pl.semaphore_wait(barrier, n - 1)

    def gathered(src, ss, dev):
        return remote(allr.at[src], allr.at[src], ss, ag_r.at[src], dev)

    direct = [gathered(me, ag_s.at[0], partner)]
    for o in range(1, chips):
        direct.append(gathered(me, ag_s.at[o], lax.rem(z + o, chips) * CORES + c))
    for copy in direct[1:] + direct[:1]:
        copy.start()
    load_copies = []
    for o in range(1, n):
        copy = remote(loads.at[me], loads.at[me], l_s.at[o], l_r.at[me], lax.rem(me + o, n))
        copy.start()
        load_copies.append(copy)
    payload = remote(pay_hbm, arr_hbm, pay_s.at[0], pay_r.at[0], lax.rem(me + n // 2, n))
    payload.start()

    q_copy.wait()
    cache_copy.wait()

    def attend(r):
        latent = cache_v[r]
        scores = lax.dot_general(q_v[r], latent, (((1,), (1,)), ((), ())),
                                 preferred_element_type=jnp.float32) * softmax_scale
        slots = lax.broadcasted_iota(jnp.int32, scores.shape, 1)
        included = slots < len_ref[me * rows + r]
        scores = jnp.where(included, scores, jnp.float32(-1e30))
        top = jnp.max(scores, axis=-1, keepdims=True)
        weights = jnp.where(included, jnp.exp(scores - top), jnp.float32(0.0))
        total = jnp.sum(weights, axis=-1, keepdims=True)
        summed = jnp.dot(weights.astype(jnp.bfloat16), latent[:, :VL],
                         preferred_element_type=jnp.float32)
        attn_ref[r] = (summed / total).astype(jnp.bfloat16)

    attend(0)

    forwards = []
    for o in range(1, chips):
        src = lax.rem(z + chips - o, chips) * CORES + c
        gathered(src, ag_s.at[o], partner).wait_recv()
        copy = gathered(src, fw_s.at[o], partner)
        copy.start()
        forwards.append(copy)
    gathered(partner, ag_s.at[0], partner).wait_recv()
    for o in range(1, chips):
        src = lax.rem(z + chips - o, chips) * CORES + (1 - c)
        gathered(src, fw_s.at[o], partner).wait_recv()

    for d in range(n):
        at = ((d % CORES) * chips + d // CORES) * rows
        xs[at:at + rows, :] = allr[d].astype(jnp.float32)
    x_v[...] = xs[...].astype(jnp.bfloat16)

    def up_step(i, carry):
        up_copy(i).wait()
        up = jnp.dot(x_v[...], wu_v[i], preferred_element_type=jnp.float32)
        hidden_v[i] = (up / (1.0 + jnp.exp(-up))).astype(jnp.bfloat16)
        return carry

    lax.fori_loop(0, nu, up_step, 0)

    def swap(i):
        return remote(part.at[1 - c, i], rx1.at[i], s1.at[i], r1.at[i], partner)

    def scatter(i, o):
        to = lax.rem(z + o, chips)
        return remote(red.at[i, to], rx2.at[i, z], s2.at[i, o], r2.at[i, z], to * CORES + c)

    def reduce_step(i):
        swap(i).wait_recv()
        both = part[c, i] + rx1[i]
        for t in range(chips):
            red[i, t] = both[t * rows:(t + 1) * rows, :]
        for o in range(1, chips):
            scatter(i, o).start()

    def down_step(i, carry):
        down_copy(i).wait()
        acc = jnp.zeros((n * rows, cd), jnp.float32)
        for k in range(nu):
            acc = acc + jnp.dot(hidden_v[k], wd_v[i, k * cu:(k + 1) * cu, :],
                                preferred_element_type=jnp.float32)
        part[0, i] = acc[:half_rows]
        part[1, i] = acc[half_rows:]
        swap(i).start()

        @pl.when(i > 0)
        def _():
            reduce_step(i - 1)

        return carry

    lax.fori_loop(0, nd, down_step, 0)
    reduce_step(nd - 1)

    for r in range(1, rows):
        attend(r)

    for o in range(1, n):
        src = lax.rem(me + o, n)
        remote(loads.at[src], loads.at[src], l_s.at[o], l_r.at[src], src).wait_recv()
    total_load = loads[0]
    for d in range(1, n):
        total_load = total_load + loads[d]
    load_ref[...] = total_load

    def finish(i, carry):
        acc = red[i, z]
        for o in range(1, chips):
            src = lax.rem(z + o, chips)
            remote(red.at[i, src], rx2.at[i, src], s2.at[i, o], r2.at[i, src],
                   src * CORES + c).wait_recv()
            acc = acc + rx2[i, src]
        cols = pl.ds(pl.multiple_of(i * cd, 128), cd)
        mixed_ref[:, cols] = (hid_ref[:, cols].astype(jnp.float32) + acc).astype(jnp.bfloat16)
        return carry

    lax.fori_loop(0, nd, finish, 0)

    def drain(i, carry):
        swap(i).wait_send()
        for o in range(1, chips):
            scatter(i, o).wait_send()
        return carry

    lax.fori_loop(0, nd, drain, 0)
    for copy in direct + forwards + load_copies:
        copy.wait_send()
    payload.wait()


def chunk_of(size, most):
    return max(w for w in range(128, most + 1, 128) if size % w == 0)


def fused(n, q_lat, latent_cache, lengths, hidden_in, gain, w_up, w_down, counts, deadline, payload):
    rows, dim = hidden_in.shape
    units = w_up.shape[1]
    heads, width = q_lat.shape[1:]
    context = latent_cache.shape[1]
    chips = n // CORES
    cu, cd = chunk_of(units, 256), chunk_of(dim, 512)
    nu, nd = units // cu, dim // cd
    bf, f32 = jnp.bfloat16, jnp.float32
    vmem, smem = pltpu.VMEM, pltpu.SMEM
    dma = pltpu.SemaphoreType.DMA

    def spec(space):
        return pl.BlockSpec(memory_space=space)

    return pl.pallas_call(
        functools.partial(body, n),
        name="fused",
        out_shape=(
            jax.ShapeDtypeStruct((rows, heads, VL), bf),
            jax.ShapeDtypeStruct((context, width), bf),
            jax.ShapeDtypeStruct((rows, dim), bf),
            jax.ShapeDtypeStruct((1, 128), f32),
        ),
        in_specs=[spec(pl.ANY), spec(pl.ANY), spec(smem), spec(vmem), spec(vmem), spec(pl.ANY),
                  spec(pl.ANY), spec(vmem), spec(smem), spec(pl.ANY)],
        out_specs=(spec(vmem), spec(pl.ANY), spec(vmem), spec(vmem)),
        scratch_shapes=[
            vmem((rows, heads, width), bf),
            vmem((rows, context, width), bf),
            vmem((nu, dim, cu), bf),
            vmem((nd, units, cd), bf),
            vmem((n, rows, dim), bf),
            vmem((n * rows, dim), f32),
            vmem((n * rows, dim), bf),
            vmem((nu, n * rows, cu), bf),
            vmem((CORES, nd, chips * rows, cd), f32),
            vmem((nd, chips * rows, cd), f32),
            vmem((nd, chips, rows, cd), f32),
            vmem((nd, chips, rows, cd), f32),
            vmem((n, 1, 128), f32),
            dma((2,)), dma((nu,)), dma((nd,)),
            dma((chips,)), dma((n,)), dma((chips,)),
            dma((1,)), dma((1,)),
            dma((nd,)), dma((nd,)), dma((nd, chips)), dma((nd, chips)),
            dma((n,)), dma((n,)),
        ],
        compiler_params=pltpu.CompilerParams(
            collective_id=0, has_side_effects=True, vmem_limit_bytes=48 << 20),
    )(q_lat, latent_cache, lengths, hidden_in, gain, w_up, w_down, counts, deadline, payload)


def shifted(value, steps):
    count = lax.axis_size("dev")
    pairs = [(source, (source + steps) % count) for source in range(count)]
    return lax.ppermute(value, "dev", pairs)


def per_device(
    q_lat, latent_cache, lengths, moves, hidden_in, norm_gain, w_up, w_down, queue_counts, deadline
):
    devices = lax.axis_size("dev")
    me = lax.axis_index("dev")
    row_count = latent_cache.shape[0]
    own = lax.dynamic_index_in_dim(moves.reshape(MOVE_DEV, devices, 3), me, 1, keepdims=False)
    leaving = own[:, 0] - me * row_count
    distance = (own[:, 2] - me) % devices
    first_is_half = distance[0] == devices // 2
    half_row = jnp.where(first_is_half, leaving[0], leaving[1])
    other_row = jnp.where(first_is_half, leaving[1], leaving[0])
    other_distance = jnp.where(first_is_half, distance[1], distance[0])
    half_payload = lax.dynamic_index_in_dim(latent_cache, half_row, 0, keepdims=False)
    other_payload = lax.dynamic_index_in_dim(latent_cache, other_row, 0, keepdims=False)
    branches = [functools.partial(lambda o, v: shifted(v, o), o) for o in range(1, devices)]
    other_arrival = lax.switch(other_distance - 1, branches, other_payload)
    counts = jnp.pad(queue_counts, ((0, 0), (0, 128 - BUCKETS)))
    attn_out, half_arrival, mixed, load = fused(
        devices, q_lat, latent_cache, lengths, hidden_in, norm_gain[None, :], w_up, w_down,
        counts, deadline, half_payload)
    slot = jnp.arange(row_count, dtype=jnp.int32)[:, None, None]
    new_cache = jnp.where(
        slot == half_row, half_arrival[None],
        jnp.where(slot == other_row, other_arrival[None], latent_cache))
    return (attn_out, new_cache, mixed, load[0, :BUCKETS])


def solution(mesh):
    return jax.shard_map(
        per_device,
        mesh=mesh,
        in_specs=(
            P(("grp", "dev"), None, None),
            P(("grp", "dev"), None, None),
            P("grp"),
            P("grp", None),
            P(("grp", "dev"), None),
            P(),
            P(None, "dev"),
            P("dev", None),
            P(("grp", "dev"), None),
            P(("grp", "dev")),
        ),
        out_specs=(
            P(("grp", "dev"), None, None),
            P(("grp", "dev"), None, None),
            P(("grp", "dev"), None),
            P("grp"),
        ),
        check_vma=False,
    )
```

```python
import functools

import jax
import jax.numpy as jnp
from jax import lax
from jax.experimental import pallas as pl
from jax.experimental.pallas import tpu as pltpu
from jax.sharding import PartitionSpec as P

VL = 512
MOVE_DEV = 2
BUCKETS = 8
CORES = 2
MESH = pl.DeviceIdType.MESH

softmax_scale = 192.0 ** (-0.5)


def body(
    n,
    q_hbm, cache_hbm, len_ref, hid_ref, gain_ref, wu_hbm, wd_hbm, qc_ref, dl_ref, pay_hbm,
    attn_ref, arr_hbm, mixed_ref, load_ref,
    q_v, cache_v, wu_v, wd_v, allr, xs, x_v, hidden_v, part, rx1, red, rx2, loads,
    sem_in, sem_wu, sem_wd, ag_s, ag_r, fw_s, pay_s, pay_r, s1, r1, s2, r2, l_s, l_r,
):
    me = lax.axis_index("dev")
    chips = n // CORES
    z, c = me // CORES, me % CORES
    partner = z * CORES + (1 - c)
    rows, dim = hid_ref.shape
    nu, nd = wu_v.shape[0], wd_v.shape[0]
    cu, cd = wu_v.shape[2], wd_v.shape[2]
    half_rows = chips * rows

    def remote(src, dst, ss, rs, dev):
        return pltpu.make_async_remote_copy(
            src_ref=src, dst_ref=dst, send_sem=ss, recv_sem=rs,
            device_id={"dev": dev}, device_id_type=MESH)

    def up_copy(i):
        return pltpu.make_async_copy(
            wu_hbm.at[:, pl.ds(pl.multiple_of(i * cu, 128), cu)], wu_v.at[i], sem_wu.at[i])

    def down_copy(i):
        return pltpu.make_async_copy(
            wd_hbm.at[:, pl.ds(pl.multiple_of(i * cd, 128), cd)], wd_v.at[i], sem_wd.at[i])

    barrier = pltpu.get_barrier_semaphore()
    for o in range(1, n):
        pl.semaphore_signal(barrier, inc=1, device_id={"dev": lax.rem(me + o, n)},
                            device_id_type=MESH)
    q_copy = pltpu.make_async_copy(q_hbm, q_v, sem_in.at[0])
    cache_copy = pltpu.make_async_copy(cache_hbm, cache_v, sem_in.at[1])
    q_copy.start()
    cache_copy.start()
    for i in range(nu):
        up_copy(i).start()
    for i in range(nd):
        down_copy(i).start()

    widened = hid_ref[...].astype(jnp.float32)
    scaled = lax.rsqrt(jnp.mean(widened * widened, axis=-1, keepdims=True) + 1e-06)
    normed = widened * scaled * gain_ref[...].astype(jnp.float32).reshape(1, dim)
    allr[me] = normed.astype(jnp.bfloat16)
    buckets = lax.broadcasted_iota(jnp.int32, (1, BUCKETS), 1)
    counted = qc_ref[...].astype(jnp.float32)
    for r in range(rows):
        counted = counted + jnp.where(buckets == dl_ref[r], 1.0, 0.0)
    loads[me] = jnp.zeros((1, 128), jnp.float32)
    loads[me, :, 0:BUCKETS] = counted
    pl.semaphore_wait(barrier, n - 1)

    def gathered(src, ss, dev):
        return remote(allr.at[src], allr.at[src], ss, ag_r.at[src], dev)

    direct = [gathered(me, ag_s.at[0], partner)]
    for o in range(1, chips):
        direct.append(gathered(me, ag_s.at[o], lax.rem(z + o, chips) * CORES + c))
    for copy in direct[1:] + direct[:1]:
        copy.start()
    load_copies = []
    for o in range(1, n):
        copy = remote(loads.at[me], loads.at[me], l_s.at[o], l_r.at[me], lax.rem(me + o, n))
        copy.start()
        load_copies.append(copy)
    payload = remote(pay_hbm, arr_hbm, pay_s.at[0], pay_r.at[0], lax.rem(me + n // 2, n))
    payload.start()

    q_copy.wait()
    cache_copy.wait()

    def attend(r):
        latent = cache_v[r]
        scores = jnp.dot(q_v[r], latent, preferred_element_type=jnp.float32) * softmax_scale
        slots = lax.broadcasted_iota(jnp.int32, scores.shape, 1)
        included = slots < len_ref[me * rows + r]
        scores = jnp.where(included, scores, jnp.float32(-1e30))
        top = jnp.max(scores, axis=-1, keepdims=True)
        weights = jnp.where(included, jnp.exp(scores - top), jnp.float32(0.0))
        total = jnp.sum(weights, axis=-1, keepdims=True)
        summed = lax.dot_general(weights.astype(jnp.bfloat16), latent[:VL, :],
                                 (((1,), (1,)), ((), ())), preferred_element_type=jnp.float32)
        attn_ref[r] = (summed / total).astype(jnp.bfloat16)

    attend(0)

    forwards = []
    for o in range(1, chips):
        src = lax.rem(z + chips - o, chips) * CORES + c
        gathered(src, ag_s.at[o], partner).wait_recv()
        copy = gathered(src, fw_s.at[o], partner)
        copy.start()
        forwards.append(copy)
    gathered(partner, ag_s.at[0], partner).wait_recv()
    for o in range(1, chips):
        src = lax.rem(z + chips - o, chips) * CORES + (1 - c)
        gathered(src, fw_s.at[o], partner).wait_recv()

    for d in range(n):
        at = ((d % CORES) * chips + d // CORES) * rows
        xs[at:at + rows, :] = allr[d].astype(jnp.float32)
    x_v[...] = xs[...].astype(jnp.bfloat16)

    def up_step(i, carry):
        up_copy(i).wait()
        up = jnp.dot(x_v[...], wu_v[i], preferred_element_type=jnp.float32)
        hidden_v[i] = (up / (1.0 + jnp.exp(-up))).astype(jnp.bfloat16)
        return carry

    lax.fori_loop(0, nu, up_step, 0)

    def swap(i):
        return remote(part.at[1 - c, i], rx1.at[i], s1.at[i], r1.at[i], partner)

    def scatter(i, o):
        to = lax.rem(z + o, chips)
        return remote(red.at[i, to], rx2.at[i, z], s2.at[i, o], r2.at[i, z], to * CORES + c)

    def reduce_step(i):
        swap(i).wait_recv()
        both = part[c, i] + rx1[i]
        for t in range(chips):
            red[i, t] = both[t * rows:(t + 1) * rows, :]
        for o in range(1, chips):
            scatter(i, o).start()

    def down_step(i, carry):
        down_copy(i).wait()
        acc = jnp.zeros((n * rows, cd), jnp.float32)
        for k in range(nu):
            acc = acc + jnp.dot(hidden_v[k], wd_v[i, k * cu:(k + 1) * cu, :],
                                preferred_element_type=jnp.float32)
        part[0, i] = acc[:half_rows]
        part[1, i] = acc[half_rows:]
        swap(i).start()

        @pl.when(i > 0)
        def _():
            reduce_step(i - 1)

        return carry

    lax.fori_loop(0, nd, down_step, 0)
    reduce_step(nd - 1)

    for r in range(1, rows):
        attend(r)

    for o in range(1, n):
        src = lax.rem(me + o, n)
        remote(loads.at[src], loads.at[src], l_s.at[o], l_r.at[src], src).wait_recv()
    total_load = loads[0]
    for d in range(1, n):
        total_load = total_load + loads[d]
    load_ref[...] = total_load[:, 0:BUCKETS]

    def finish(i, carry):
        acc = red[i, z]
        for o in range(1, chips):
            src = lax.rem(z + o, chips)
            remote(red.at[i, src], rx2.at[i, src], s2.at[i, o], r2.at[i, src],
                   src * CORES + c).wait_recv()
            acc = acc + rx2[i, src]
        cols = pl.ds(pl.multiple_of(i * cd, 128), cd)
        mixed_ref[:, cols] = (hid_ref[:, cols].astype(jnp.float32) + acc).astype(jnp.bfloat16)
        return carry

    lax.fori_loop(0, nd, finish, 0)

    def drain(i, carry):
        swap(i).wait_send()
        for o in range(1, chips):
            scatter(i, o).wait_send()
        return carry

    lax.fori_loop(0, nd, drain, 0)
    for copy in direct + forwards + load_copies:
        copy.wait_send()
    payload.wait()


def chunk_of(size, most):
    return max(w for w in range(128, most + 1, 128) if size % w == 0)


def fused(n, q_lat, latent_cache, lengths, hidden_in, gain, w_up, w_down, counts, deadline, payload):
    rows, dim = hidden_in.shape
    units = w_up.shape[1]
    heads, width = q_lat.shape[1:]
    context = latent_cache.shape[2]
    chips = n // CORES
    cu, cd = chunk_of(units, 256), chunk_of(dim, 512)
    nu, nd = units // cu, dim // cd
    bf, f32 = jnp.bfloat16, jnp.float32
    vmem, smem = pltpu.VMEM, pltpu.SMEM
    dma = pltpu.SemaphoreType.DMA

    def spec(space):
        return pl.BlockSpec(memory_space=space)

    return pl.pallas_call(
        functools.partial(body, n),
        name="fused",
        out_shape=(
            jax.ShapeDtypeStruct((rows, heads, VL), bf),
            jax.ShapeDtypeStruct((width, context), bf),
            jax.ShapeDtypeStruct((rows, dim), bf),
            jax.ShapeDtypeStruct((1, BUCKETS), f32),
        ),
        in_specs=[spec(pl.ANY), spec(pl.ANY), spec(smem), spec(vmem), spec(vmem), spec(pl.ANY),
                  spec(pl.ANY), spec(vmem), spec(smem), spec(pl.ANY)],
        out_specs=(spec(vmem), spec(pl.ANY), spec(vmem), spec(vmem)),
        scratch_shapes=[
            vmem((rows, heads, width), bf),
            vmem((rows, width, context), bf),
            vmem((nu, dim, cu), bf),
            vmem((nd, units, cd), bf),
            vmem((n, rows, dim), bf),
            vmem((n * rows, dim), f32),
            vmem((n * rows, dim), bf),
            vmem((nu, n * rows, cu), bf),
            vmem((CORES, nd, chips * rows, cd), f32),
            vmem((nd, chips * rows, cd), f32),
            vmem((nd, chips, rows, cd), f32),
            vmem((nd, chips, rows, cd), f32),
            vmem((n, 1, 128), f32),
            dma((2,)), dma((nu,)), dma((nd,)),
            dma((chips,)), dma((n,)), dma((chips,)),
            dma((1,)), dma((1,)),
            dma((nd,)), dma((nd,)), dma((nd, chips)), dma((nd, chips)),
            dma((n,)), dma((n,)),
        ],
        compiler_params=pltpu.CompilerParams(
            collective_id=0, has_side_effects=True, vmem_limit_bytes=48 << 20),
    )(q_lat, latent_cache, lengths, hidden_in, gain, w_up, w_down, counts, deadline, payload)


def pick(n, moves_ref, lat_hbm, half_ref, other_ref, info_ref, sems):
    me = lax.axis_index("dev")
    rows = lat_hbm.shape[0]
    row_a = moves_ref[0, me] - me * rows
    row_b = moves_ref[0, n + me] - me * rows
    hop_a = lax.rem(moves_ref[2, me] - me + n, n)
    hop_b = lax.rem(moves_ref[2, n + me] - me + n, n)
    first = hop_a == n // 2
    half_row = jnp.where(first, row_a, row_b)
    other_row = jnp.where(first, row_b, row_a)
    half_copy = pltpu.make_async_copy(lat_hbm.at[half_row], half_ref, sems.at[0])
    other_copy = pltpu.make_async_copy(lat_hbm.at[other_row], other_ref, sems.at[1])
    other_copy.start()
    half_copy.start()
    info_ref[0] = jnp.where(first, hop_b, hop_a) - 1
    info_ref[1] = half_row
    info_ref[2] = other_row
    other_copy.wait()
    half_copy.wait()


def picked(n, moves, latent):
    slot = jax.ShapeDtypeStruct(latent.shape[1:], latent.dtype)
    vmem = pl.BlockSpec(memory_space=pltpu.VMEM)
    smem = pl.BlockSpec(memory_space=pltpu.SMEM)
    return pl.pallas_call(
        functools.partial(pick, n),
        name="pick",
        out_shape=(slot, slot, jax.ShapeDtypeStruct((3,), jnp.int32)),
        in_specs=[smem, pl.BlockSpec(memory_space=pl.ANY)],
        out_specs=(vmem, vmem, smem),
        scratch_shapes=[pltpu.SemaphoreType.DMA((2,))],
    )(moves, latent)


def settle(info_ref, lat_hbm, half_ref, other_ref, attn_ref, mixed_ref,
           cache_out, attn_out, mixed_out, kept, sem_in, sem_out):
    rows = lat_hbm.shape[0]
    half_row, other_row = info_ref[1], info_ref[2]

    def stays(r):
        return jnp.logical_and(half_row != r, other_row != r)

    def fetch(r):
        return pltpu.make_async_copy(lat_hbm.at[r], kept.at[r], sem_in.at[r])

    def put(r):
        return pltpu.make_async_copy(kept.at[r], cache_out.at[r], sem_out.at[r])

    for r in range(rows):
        pl.when(stays(r))(lambda r=r: fetch(r).start())
    outs = [
        pltpu.make_async_copy(half_ref, cache_out.at[half_row], sem_out.at[rows]),
        pltpu.make_async_copy(other_ref, cache_out.at[other_row], sem_out.at[rows + 1]),
        pltpu.make_async_copy(attn_ref, attn_out, sem_out.at[rows + 2]),
        pltpu.make_async_copy(mixed_ref, mixed_out, sem_out.at[rows + 3]),
    ]
    for copy in outs:
        copy.start()
    for r in range(rows):
        @pl.when(stays(r))
        def _(r=r):
            fetch(r).wait()
            put(r).start()
    for r in range(rows):
        pl.when(stays(r))(lambda r=r: put(r).wait())
    for copy in outs:
        copy.wait()


def settled(info, latent, half, other, attn, mixed):
    rows = latent.shape[0]
    vmem = pl.BlockSpec(memory_space=pltpu.VMEM)
    hbm = pl.BlockSpec(memory_space=pl.ANY)
    like = jax.ShapeDtypeStruct
    return pl.pallas_call(
        settle,
        name="settle",
        out_shape=(like(latent.shape, latent.dtype), like(attn.shape, attn.dtype),
                   like(mixed.shape, mixed.dtype)),
        in_specs=[pl.BlockSpec(memory_space=pltpu.SMEM), hbm, vmem, vmem, vmem, vmem],
        out_specs=(hbm, hbm, hbm),
        scratch_shapes=[
            pltpu.VMEM(latent.shape, latent.dtype),
            pltpu.SemaphoreType.DMA((rows,)), pltpu.SemaphoreType.DMA((rows + 4,)),
        ],
    )(info, latent, half, other, attn, mixed)


def shifted(value, steps):
    count = lax.axis_size("dev")
    pairs = [(source, (source + steps) % count) for source in range(count)]
    return lax.ppermute(value, "dev", pairs)


def per_device(
    q_lat, latent_cache, lengths, moves, hidden_in, norm_gain, w_up, w_down, queue_counts, deadline
):
    devices = lax.axis_size("dev")
    latent = jnp.swapaxes(latent_cache, 1, 2)
    half_payload, other_payload, info = picked(devices, moves.T, latent)
    branches = [functools.partial(lambda o, v: shifted(v, o), o) for o in range(1, devices)]
    other_arrival = lax.switch(info[0], branches, other_payload)
    attn, half_arrival, mixed, load = fused(
        devices, q_lat, latent, lengths, hidden_in, norm_gain, w_up, w_down,
        queue_counts, deadline, half_payload)
    new_cache, attn_out, mixed_out = settled(
        info, latent, half_arrival, other_arrival, attn, mixed)
    return (attn_out, jnp.swapaxes(new_cache, 1, 2), mixed_out, load[0])


def solution(mesh):
    return jax.shard_map(
        per_device,
        mesh=mesh,
        in_specs=(
            P(("grp", "dev"), None, None),
            P(("grp", "dev"), None, None),
            P("grp"),
            P("grp", None),
            P(("grp", "dev"), None),
            P(),
            P(None, "dev"),
            P("dev", None),
            P(("grp", "dev"), None),
            P(("grp", "dev")),
        ),
        out_specs=(
            P(("grp", "dev"), None, None),
            P(("grp", "dev"), None, None),
            P(("grp", "dev"), None),
            P("grp"),
        ),
        check_vma=False,
    )
```

```python
import functools

import jax
import jax.numpy as jnp
from jax import lax
from jax.experimental import pallas as pl
from jax.experimental.pallas import tpu as pltpu
from jax.sharding import PartitionSpec as P

VL = 512
MOVE_DEV = 2
BUCKETS = 8
CORES = 2
GRANT = 67043328
MESH = pl.DeviceIdType.MESH

softmax_scale = 192.0 ** (-0.5)


def body(
    n,
    q_hbm, cache_hbm, len_ref, hid_ref, gain_ref, wu_hbm, wd_hbm, qc_ref, dl_ref, pay_hbm,
    attn_ref, arr_hbm, mixed_ref, load_ref,
    q_v, cache_v, wu_v, wd_v, allr, xs, x_v, hidden_v, part, rx1, red, rx2, loads,
    sem_in, sem_wu, sem_wd, ag_s, ag_r, fw_s, pay_s, pay_r, s1, r1, s2, r2, l_s, l_r,
):
    me = lax.axis_index("dev")
    chips = n // CORES
    z, c = me // CORES, me % CORES
    partner = z * CORES + (1 - c)
    rows, dim = hid_ref.shape
    nu, nd = wu_v.shape[0], wd_v.shape[0]
    cu, cd = wu_v.shape[2], wd_v.shape[2]
    half_rows = chips * rows

    def remote(src, dst, ss, rs, dev):
        return pltpu.make_async_remote_copy(
            src_ref=src, dst_ref=dst, send_sem=ss, recv_sem=rs,
            device_id={"dev": dev}, device_id_type=MESH)

    def up_copy(i):
        return pltpu.make_async_copy(
            wu_hbm.at[:, pl.ds(pl.multiple_of(i * cu, 128), cu)], wu_v.at[i], sem_wu.at[i])

    def down_copy(i):
        return pltpu.make_async_copy(
            wd_hbm.at[:, pl.ds(pl.multiple_of(i * cd, 128), cd)], wd_v.at[i], sem_wd.at[i])

    barrier = pltpu.get_barrier_semaphore()
    for o in range(1, n):
        pl.semaphore_signal(barrier, inc=1, device_id={"dev": lax.rem(me + o, n)},
                            device_id_type=MESH)
    q_copy = pltpu.make_async_copy(q_hbm, q_v, sem_in.at[0])
    cache_copy = pltpu.make_async_copy(cache_hbm, cache_v, sem_in.at[1])
    q_copy.start()
    cache_copy.start()
    for i in range(nu):
        up_copy(i).start()
    for i in range(nd):
        down_copy(i).start()

    widened = hid_ref[...].astype(jnp.float32)
    scaled = lax.rsqrt(jnp.mean(widened * widened, axis=-1, keepdims=True) + 1e-06)
    normed = widened * scaled * gain_ref[...].astype(jnp.float32).reshape(1, dim)
    allr[me] = normed.astype(jnp.bfloat16)
    buckets = lax.broadcasted_iota(jnp.int32, (1, BUCKETS), 1)
    counted = qc_ref[...].astype(jnp.float32)
    for r in range(rows):
        counted = counted + jnp.where(buckets == dl_ref[r], 1.0, 0.0)
    loads[me] = jnp.zeros((1, 128), jnp.float32)
    loads[me, :, 0:BUCKETS] = counted
    pl.semaphore_wait(barrier, n - 1)

    def gathered(src, ss, dev):
        return remote(allr.at[src], allr.at[src], ss, ag_r.at[src], dev)

    direct = [gathered(me, ag_s.at[0], partner)]
    for o in range(1, chips):
        direct.append(gathered(me, ag_s.at[o], lax.rem(z + o, chips) * CORES + c))
    for copy in direct[1:] + direct[:1]:
        copy.start()
    load_copies = []
    for o in range(1, n):
        copy = remote(loads.at[me], loads.at[me], l_s.at[o], l_r.at[me], lax.rem(me + o, n))
        copy.start()
        load_copies.append(copy)
    payload = remote(pay_hbm, arr_hbm, pay_s.at[0], pay_r.at[0], lax.rem(me + n // 2, n))
    payload.start()

    q_copy.wait()
    cache_copy.wait()

    def attend(r):
        latent = cache_v[r]
        scores = jnp.dot(q_v[r], latent, preferred_element_type=jnp.float32) * softmax_scale
        slots = lax.broadcasted_iota(jnp.int32, scores.shape, 1)
        included = slots < len_ref[me * rows + r]
        scores = jnp.where(included, scores, jnp.float32(-1e30))
        top = jnp.max(scores, axis=-1, keepdims=True)
        weights = jnp.where(included, jnp.exp(scores - top), jnp.float32(0.0))
        total = jnp.sum(weights, axis=-1, keepdims=True)
        summed = lax.dot_general(weights.astype(jnp.bfloat16), latent[:VL, :],
                                 (((1,), (1,)), ((), ())), preferred_element_type=jnp.float32)
        attn_ref[r] = (summed / total).astype(jnp.bfloat16)

    attend(0)

    forwards = []
    for o in range(1, chips):
        src = lax.rem(z + chips - o, chips) * CORES + c
        gathered(src, ag_s.at[o], partner).wait_recv()
        copy = gathered(src, fw_s.at[o], partner)
        copy.start()
        forwards.append(copy)
    gathered(partner, ag_s.at[0], partner).wait_recv()
    for o in range(1, chips):
        src = lax.rem(z + chips - o, chips) * CORES + (1 - c)
        gathered(src, fw_s.at[o], partner).wait_recv()

    for d in range(n):
        at = ((d % CORES) * chips + d // CORES) * rows
        xs[at:at + rows, :] = allr[d].astype(jnp.float32)
    x_v[...] = xs[...].astype(jnp.bfloat16)

    def up_step(i, carry):
        up_copy(i).wait()
        up = jnp.dot(x_v[...], wu_v[i], preferred_element_type=jnp.float32)
        hidden_v[i] = (up / (1.0 + jnp.exp(-up))).astype(jnp.bfloat16)
        return carry

    lax.fori_loop(0, nu, up_step, 0)

    def swap(i):
        return remote(part.at[1 - c, i], rx1.at[i], s1.at[i], r1.at[i], partner)

    def scatter(i, o):
        to = lax.rem(z + o, chips)
        return remote(red.at[i, to], rx2.at[i, z], s2.at[i, o], r2.at[i, z], to * CORES + c)

    def reduce_step(i):
        swap(i).wait_recv()
        both = part[c, i] + rx1[i]
        for t in range(chips):
            red[i, t] = both[t * rows:(t + 1) * rows, :]
        for o in range(1, chips):
            scatter(i, o).start()

    def down_step(i, carry):
        down_copy(i).wait()
        acc = jnp.zeros((n * rows, cd), jnp.float32)
        for k in range(nu):
            acc = acc + jnp.dot(hidden_v[k], wd_v[i, k * cu:(k + 1) * cu, :],
                                preferred_element_type=jnp.float32)
        part[0, i] = acc[:half_rows]
        part[1, i] = acc[half_rows:]
        swap(i).start()

        @pl.when(i > 0)
        def _():
            reduce_step(i - 1)

        return carry

    lax.fori_loop(0, nd, down_step, 0)
    reduce_step(nd - 1)

    for r in range(1, rows):
        attend(r)

    for o in range(1, n):
        src = lax.rem(me + o, n)
        remote(loads.at[src], loads.at[src], l_s.at[o], l_r.at[src], src).wait_recv()
    total_load = loads[0]
    for d in range(1, n):
        total_load = total_load + loads[d]
    load_ref[...] = total_load[:, 0:BUCKETS]

    def finish(i, carry):
        acc = red[i, z]
        for o in range(1, chips):
            src = lax.rem(z + o, chips)
            remote(red.at[i, src], rx2.at[i, src], s2.at[i, o], r2.at[i, src],
                   src * CORES + c).wait_recv()
            acc = acc + rx2[i, src]
        cols = pl.ds(pl.multiple_of(i * cd, 128), cd)
        mixed_ref[:, cols] = (hid_ref[:, cols].astype(jnp.float32) + acc).astype(jnp.bfloat16)
        return carry

    lax.fori_loop(0, nd, finish, 0)

    def drain(i, carry):
        swap(i).wait_send()
        for o in range(1, chips):
            scatter(i, o).wait_send()
        return carry

    lax.fori_loop(0, nd, drain, 0)
    for copy in direct + forwards + load_copies:
        copy.wait_send()
    payload.wait()


def chunk_of(size, most):
    return max(w for w in range(128, most + 1, 128) if size % w == 0)


def fused(n, q_lat, latent_cache, lengths, hidden_in, gain, w_up, w_down, counts, deadline, payload):
    rows, dim = hidden_in.shape
    units = w_up.shape[1]
    heads, width = q_lat.shape[1:]
    context = latent_cache.shape[2]
    chips = n // CORES
    cu, cd = chunk_of(units, 256), chunk_of(dim, 512)
    nu, nd = units // cu, dim // cd
    bf, f32 = jnp.bfloat16, jnp.float32
    vmem, smem = pltpu.VMEM, pltpu.SMEM
    dma = pltpu.SemaphoreType.DMA

    def spec(space):
        return pl.BlockSpec(memory_space=space)

    return pl.pallas_call(
        functools.partial(body, n),
        name="fused",
        out_shape=(
            jax.ShapeDtypeStruct((rows, heads, VL), bf),
            jax.ShapeDtypeStruct((width, context), bf),
            jax.ShapeDtypeStruct((rows, dim), bf),
            jax.ShapeDtypeStruct((1, BUCKETS), f32),
        ),
        in_specs=[spec(pl.ANY), spec(pl.ANY), spec(smem), spec(vmem), spec(vmem), spec(pl.ANY),
                  spec(pl.ANY), spec(vmem), spec(smem), spec(pl.ANY)],
        out_specs=(spec(vmem), spec(pl.ANY), spec(vmem), spec(vmem)),
        scratch_shapes=[
            vmem((rows, heads, width), bf),
            vmem((rows, width, context), bf),
            vmem((nu, dim, cu), bf),
            vmem((nd, units, cd), bf),
            vmem((n, rows, dim), bf),
            vmem((n * rows, dim), f32),
            vmem((n * rows, dim), bf),
            vmem((nu, n * rows, cu), bf),
            vmem((CORES, nd, chips * rows, cd), f32),
            vmem((nd, chips * rows, cd), f32),
            vmem((nd, chips, rows, cd), f32),
            vmem((nd, chips, rows, cd), f32),
            vmem((n, 1, 128), f32),
            dma((2,)), dma((nu,)), dma((nd,)),
            dma((chips,)), dma((n,)), dma((chips,)),
            dma((1,)), dma((1,)),
            dma((nd,)), dma((nd,)), dma((nd, chips)), dma((nd, chips)),
            dma((n,)), dma((n,)),
        ],
        compiler_params=pltpu.CompilerParams(
            collective_id=0, has_side_effects=True, vmem_limit_bytes=GRANT),
    )(q_lat, latent_cache, lengths, hidden_in, gain, w_up, w_down, counts, deadline, payload)


def pick(n, moves_ref, lat_hbm, half_ref, other_ref, info_ref, sems):
    me = lax.axis_index("dev")
    rows = lat_hbm.shape[0]
    row_a = moves_ref[0, me] - me * rows
    row_b = moves_ref[0, n + me] - me * rows
    hop_a = lax.rem(moves_ref[2, me] - me + n, n)
    hop_b = lax.rem(moves_ref[2, n + me] - me + n, n)
    first = hop_a == n // 2
    half_row = jnp.where(first, row_a, row_b)
    other_row = jnp.where(first, row_b, row_a)
    half_copy = pltpu.make_async_copy(lat_hbm.at[half_row], half_ref, sems.at[0])
    other_copy = pltpu.make_async_copy(lat_hbm.at[other_row], other_ref, sems.at[1])
    other_copy.start()
    half_copy.start()
    info_ref[0] = jnp.where(first, hop_b, hop_a) - 1
    info_ref[1] = half_row
    info_ref[2] = other_row
    other_copy.wait()
    half_copy.wait()


def picked(n, moves, latent):
    slot = jax.ShapeDtypeStruct(latent.shape[1:], latent.dtype)
    vmem = pl.BlockSpec(memory_space=pltpu.VMEM)
    smem = pl.BlockSpec(memory_space=pltpu.SMEM)
    return pl.pallas_call(
        functools.partial(pick, n),
        name="pick",
        out_shape=(slot, slot, jax.ShapeDtypeStruct((3,), jnp.int32)),
        in_specs=[smem, pl.BlockSpec(memory_space=pl.ANY)],
        out_specs=(vmem, vmem, smem),
        scratch_shapes=[pltpu.SemaphoreType.DMA((2,))],
        compiler_params=pltpu.CompilerParams(vmem_limit_bytes=GRANT),
    )(moves, latent)


def settle(info_ref, lat_hbm, half_hbm, other_hbm, attn_hbm, mixed_hbm, load_hbm,
           cache_out, attn_out, mixed_out, load_out,
           kept, half_v, other_v, attn_v, mixed_v, load_v, sem_in, sem_out):
    rows = lat_hbm.shape[0]
    half_row, other_row = info_ref[1], info_ref[2]

    def stays(r):
        return jnp.logical_and(half_row != r, other_row != r)

    def fetch(r):
        return pltpu.make_async_copy(lat_hbm.at[r], kept.at[r], sem_in.at[r])

    def put(r):
        return pltpu.make_async_copy(kept.at[r], cache_out.at[r], sem_out.at[r])

    through = [
        (half_hbm, half_v, cache_out.at[half_row]),
        (other_hbm, other_v, cache_out.at[other_row]),
        (attn_hbm, attn_v, attn_out),
        (mixed_hbm, mixed_v, mixed_out),
        (load_hbm, load_v, load_out),
    ]
    ins = [pltpu.make_async_copy(a, b, sem_in.at[rows + k]) for k, (a, b, _) in enumerate(through)]
    outs = [pltpu.make_async_copy(b, o, sem_out.at[rows + k]) for k, (_, b, o) in enumerate(through)]
    for copy in ins:
        copy.start()
    for r in range(rows):
        pl.when(stays(r))(lambda r=r: fetch(r).start())
    for arrive, leave in zip(ins, outs):
        arrive.wait()
        leave.start()
    for r in range(rows):
        @pl.when(stays(r))
        def _(r=r):
            fetch(r).wait()
            put(r).start()
    for r in range(rows):
        pl.when(stays(r))(lambda r=r: put(r).wait())
    for copy in outs:
        copy.wait()


def settled(info, latent, half, other, attn, mixed, load):
    rows = latent.shape[0]
    hbm = pl.BlockSpec(memory_space=pl.ANY)

    def like(a):
        return jax.ShapeDtypeStruct(a.shape, a.dtype)

    def held(a):
        return pltpu.VMEM(a.shape, a.dtype)

    return pl.pallas_call(
        settle,
        name="settle",
        out_shape=(like(latent), like(attn), like(mixed), like(load)),
        in_specs=[pl.BlockSpec(memory_space=pltpu.SMEM)] + [hbm] * 6,
        out_specs=(hbm, hbm, hbm, hbm),
        scratch_shapes=[
            held(latent), held(half), held(other), held(attn), held(mixed), held(load),
            pltpu.SemaphoreType.DMA((rows + 5,)), pltpu.SemaphoreType.DMA((rows + 5,)),
        ],
        compiler_params=pltpu.CompilerParams(vmem_limit_bytes=GRANT),
    )(info, latent, half, other, attn, mixed, load)


def shifted(value, steps):
    count = lax.axis_size("dev")
    pairs = [(source, (source + steps) % count) for source in range(count)]
    return lax.ppermute(value, "dev", pairs)


def per_device(
    q_lat, latent_cache, lengths, moves, hidden_in, norm_gain, w_up, w_down, queue_counts, deadline
):
    devices = lax.axis_size("dev")
    latent = jnp.swapaxes(latent_cache, 1, 2)
    half_payload, other_payload, info = picked(devices, moves.T, latent)
    branches = [functools.partial(lambda o, v: shifted(v, o), o) for o in range(1, devices)]
    other_arrival = lax.switch(info[0], branches, other_payload)
    attn, half_arrival, mixed, load = fused(
        devices, q_lat, latent, lengths, hidden_in, norm_gain, w_up, w_down,
        queue_counts, deadline, half_payload)
    new_cache, attn_out, mixed_out, load_out = settled(
        info, latent, half_arrival, other_arrival, attn, mixed, load)
    return (attn_out, jnp.swapaxes(new_cache, 1, 2), mixed_out, load_out[0])


def solution(mesh):
    return jax.shard_map(
        per_device,
        mesh=mesh,
        in_specs=(
            P(("grp", "dev"), None, None),
            P(("grp", "dev"), None, None),
            P("grp"),
            P("grp", None),
            P(("grp", "dev"), None),
            P(),
            P(None, "dev"),
            P("dev", None),
            P(("grp", "dev"), None),
            P(("grp", "dev")),
        ),
        out_specs=(
            P(("grp", "dev"), None, None),
            P(("grp", "dev"), None, None),
            P(("grp", "dev"), None),
            P("grp"),
        ),
        check_vma=False,
    )
```

```python
import functools

import jax
import jax.numpy as jnp
from jax import lax
from jax.experimental import pallas as pl
from jax.experimental.pallas import tpu as pltpu
from jax.sharding import PartitionSpec as P

VL = 512
MOVE_DEV = 2
BUCKETS = 8
CORES = 2
GRANT = 67043328
MESH = pl.DeviceIdType.MESH

softmax_scale = 192.0 ** (-0.5)


def body(
    n,
    q_hbm, cache_hbm, len_ref, hid_ref, gain_ref, wu_hbm, wd_hbm, qc_ref, dl_ref, pay_hbm,
    attn_ref, arr_hbm, mixed_ref, load_ref,
    q_v, cache_v, wu_v, wd_v, allr, xs, x_v, hidden_v, part, rx1, red, rx2, loads,
    sem_in, sem_wu, sem_wd, ag_s, ag_r, fw_s, pay_s, pay_r, s1, r1, s2, r2, l_s, l_r,
):
    me = lax.axis_index("dev")
    chips = n // CORES
    z, c = me // CORES, me % CORES
    partner = z * CORES + (1 - c)
    rows, dim = hid_ref.shape
    nu, nd = wu_v.shape[0], wd_v.shape[0]
    cu, cd = wu_v.shape[2], wd_v.shape[2]
    half_rows = chips * rows

    def remote(src, dst, ss, rs, dev):
        return pltpu.make_async_remote_copy(
            src_ref=src, dst_ref=dst, send_sem=ss, recv_sem=rs,
            device_id={"dev": dev}, device_id_type=MESH)

    def up_copy(i):
        return pltpu.make_async_copy(
            wu_hbm.at[:, pl.ds(pl.multiple_of(i * cu, 128), cu)], wu_v.at[i], sem_wu.at[i])

    def down_copy(i):
        return pltpu.make_async_copy(
            wd_hbm.at[:, pl.ds(pl.multiple_of(i * cd, 128), cd)], wd_v.at[i], sem_wd.at[i])

    barrier = pltpu.get_barrier_semaphore()
    for o in range(1, n):
        pl.semaphore_signal(barrier, inc=1, device_id={"dev": lax.rem(me + o, n)},
                            device_id_type=MESH)
    q_copy = pltpu.make_async_copy(q_hbm, q_v, sem_in.at[0])
    cache_copy = pltpu.make_async_copy(cache_hbm, cache_v, sem_in.at[1])
    q_copy.start()
    cache_copy.start()
    for i in range(nu):
        up_copy(i).start()
    for i in range(nd):
        down_copy(i).start()

    widened = hid_ref[...].astype(jnp.float32)
    scaled = lax.rsqrt(jnp.mean(widened * widened, axis=-1, keepdims=True) + 1e-06)
    normed = widened * scaled * gain_ref[...].astype(jnp.float32).reshape(1, dim)
    allr[me] = normed.astype(jnp.bfloat16)
    buckets = lax.broadcasted_iota(jnp.int32, (1, BUCKETS), 1)
    counted = qc_ref[...].astype(jnp.float32)
    for r in range(rows):
        counted = counted + jnp.where(buckets == dl_ref[r], 1.0, 0.0)
    loads[me] = jnp.zeros((1, 128), jnp.float32)
    loads[me, :, 0:BUCKETS] = counted
    pl.semaphore_wait(barrier, n - 1)

    def gathered(src, ss, dev):
        return remote(allr.at[src], allr.at[src], ss, ag_r.at[src], dev)

    direct = [gathered(me, ag_s.at[0], partner)]
    for o in range(1, chips):
        direct.append(gathered(me, ag_s.at[o], lax.rem(z + o, chips) * CORES + c))
    for copy in direct[1:] + direct[:1]:
        copy.start()
    load_copies = []
    for o in range(1, n):
        copy = remote(loads.at[me], loads.at[me], l_s.at[o], l_r.at[me], lax.rem(me + o, n))
        copy.start()
        load_copies.append(copy)
    payload = remote(pay_hbm, arr_hbm, pay_s.at[0], pay_r.at[0], lax.rem(me + n // 2, n))
    payload.start()

    q_copy.wait()
    cache_copy.wait()

    def attend(r):
        latent = cache_v[r]
        scores = jnp.dot(q_v[r], latent, preferred_element_type=jnp.float32) * softmax_scale
        slots = lax.broadcasted_iota(jnp.int32, scores.shape, 1)
        included = slots < len_ref[me * rows + r]
        scores = jnp.where(included, scores, jnp.float32(-1e30))
        top = jnp.max(scores, axis=-1, keepdims=True)
        weights = jnp.where(included, jnp.exp(scores - top), jnp.float32(0.0))
        total = jnp.sum(weights, axis=-1, keepdims=True)
        summed = lax.dot_general(weights.astype(jnp.bfloat16), latent[:VL, :],
                                 (((1,), (1,)), ((), ())), preferred_element_type=jnp.float32)
        attn_ref[r] = (summed / total).astype(jnp.bfloat16)

    attend(0)

    forwards = []
    for o in range(1, chips):
        src = lax.rem(z + chips - o, chips) * CORES + c
        gathered(src, ag_s.at[o], partner).wait_recv()
        copy = gathered(src, fw_s.at[o], partner)
        copy.start()
        forwards.append(copy)
    gathered(partner, ag_s.at[0], partner).wait_recv()
    for o in range(1, chips):
        src = lax.rem(z + chips - o, chips) * CORES + (1 - c)
        gathered(src, fw_s.at[o], partner).wait_recv()

    for d in range(n):
        at = ((d % CORES) * chips + d // CORES) * rows
        xs[at:at + rows, :] = allr[d].astype(jnp.float32)
    x_v[...] = xs[...].astype(jnp.bfloat16)

    def up_step(i, carry):
        up_copy(i).wait()
        up = jnp.dot(x_v[...], wu_v[i], preferred_element_type=jnp.float32)
        hidden_v[i] = (up / (1.0 + jnp.exp(-up))).astype(jnp.bfloat16)
        return carry

    lax.fori_loop(0, nu, up_step, 0)

    def swap(i):
        return remote(part.at[1 - c, i], rx1.at[i], s1.at[i], r1.at[i], partner)

    def scatter(i, o):
        to = lax.rem(z + o, chips)
        return remote(red.at[i, to], rx2.at[i, z], s2.at[i, o], r2.at[i, z], to * CORES + c)

    def reduce_step(i):
        swap(i).wait_recv()
        both = part[c, i] + rx1[i]
        for t in range(chips):
            red[i, t] = both[t * rows:(t + 1) * rows, :]
        for o in range(1, chips):
            scatter(i, o).start()

    def down_step(i, carry):
        down_copy(i).wait()
        acc = jnp.zeros((n * rows, cd), jnp.float32)
        for k in range(nu):
            acc = acc + jnp.dot(hidden_v[k], wd_v[i, k * cu:(k + 1) * cu, :],
                                preferred_element_type=jnp.float32)
        part[0, i] = acc[:half_rows]
        part[1, i] = acc[half_rows:]
        swap(i).start()

        @pl.when(i > 0)
        def _():
            reduce_step(i - 1)

        return carry

    lax.fori_loop(0, nd, down_step, 0)
    reduce_step(nd - 1)

    for r in range(1, rows):
        attend(r)

    for o in range(1, n):
        src = lax.rem(me + o, n)
        remote(loads.at[src], loads.at[src], l_s.at[o], l_r.at[src], src).wait_recv()
    total_load = loads[0]
    for d in range(1, n):
        total_load = total_load + loads[d]
    load_ref[...] = total_load[:, 0:BUCKETS]

    def finish(i, carry):
        acc = red[i, z]
        for o in range(1, chips):
            src = lax.rem(z + o, chips)
            remote(red.at[i, src], rx2.at[i, src], s2.at[i, o], r2.at[i, src],
                   src * CORES + c).wait_recv()
            acc = acc + rx2[i, src]
        cols = pl.ds(pl.multiple_of(i * cd, 128), cd)
        mixed_ref[:, cols] = (hid_ref[:, cols].astype(jnp.float32) + acc).astype(jnp.bfloat16)
        return carry

    lax.fori_loop(0, nd, finish, 0)

    def drain(i, carry):
        swap(i).wait_send()
        for o in range(1, chips):
            scatter(i, o).wait_send()
        return carry

    lax.fori_loop(0, nd, drain, 0)
    for copy in direct + forwards + load_copies:
        copy.wait_send()
    payload.wait()


def chunk_of(size, most):
    return max(w for w in range(128, most + 1, 128) if size % w == 0)


def fused(n, q_lat, latent_cache, lengths, hidden_in, gain, w_up, w_down, counts, deadline, payload):
    rows, dim = hidden_in.shape
    units = w_up.shape[1]
    heads, width = q_lat.shape[1:]
    context = latent_cache.shape[2]
    chips = n // CORES
    cu, cd = chunk_of(units, 256), chunk_of(dim, 512)
    nu, nd = units // cu, dim // cd
    bf, f32 = jnp.bfloat16, jnp.float32
    vmem, smem = pltpu.VMEM, pltpu.SMEM
    dma = pltpu.SemaphoreType.DMA

    def spec(space):
        return pl.BlockSpec(memory_space=space)

    return pl.pallas_call(
        functools.partial(body, n),
        name="fused",
        out_shape=(
            jax.ShapeDtypeStruct((rows, heads, VL), bf),
            jax.ShapeDtypeStruct((width, context), bf),
            jax.ShapeDtypeStruct((rows, dim), bf),
            jax.ShapeDtypeStruct((1, BUCKETS), f32),
        ),
        in_specs=[spec(pl.ANY), spec(pl.ANY), spec(smem), spec(vmem), spec(vmem), spec(pl.ANY),
                  spec(pl.ANY), spec(vmem), spec(smem), spec(pl.ANY)],
        out_specs=(spec(vmem), spec(pl.ANY), spec(vmem), spec(vmem)),
        scratch_shapes=[
            vmem((rows, heads, width), bf),
            vmem((rows, width, context), bf),
            vmem((nu, dim, cu), bf),
            vmem((nd, units, cd), bf),
            vmem((n, rows, dim), bf),
            vmem((n * rows, dim), f32),
            vmem((n * rows, dim), bf),
            vmem((nu, n * rows, cu), bf),
            vmem((CORES, nd, chips * rows, cd), f32),
            vmem((nd, chips * rows, cd), f32),
            vmem((nd, chips, rows, cd), f32),
            vmem((nd, chips, rows, cd), f32),
            vmem((n, 1, 128), f32),
            dma((2,)), dma((nu,)), dma((nd,)),
            dma((chips,)), dma((n,)), dma((chips,)),
            dma((1,)), dma((1,)),
            dma((nd,)), dma((nd,)), dma((nd, chips)), dma((nd, chips)),
            dma((n,)), dma((n,)),
        ],
        compiler_params=pltpu.CompilerParams(
            collective_id=0, has_side_effects=True, vmem_limit_bytes=GRANT),
    )(q_lat, latent_cache, lengths, hidden_in, gain, w_up, w_down, counts, deadline, payload)


def pick(n, moves_ref, lat_hbm, half_ref, other_ref, info_ref, sems):
    me = lax.axis_index("dev")
    rows = lat_hbm.shape[0]
    row_a = moves_ref[0, me] - me * rows
    row_b = moves_ref[0, n + me] - me * rows
    hop_a = lax.rem(moves_ref[2, me] - me + n, n)
    hop_b = lax.rem(moves_ref[2, n + me] - me + n, n)
    first = hop_a == n // 2
    half_row = jnp.where(first, row_a, row_b)
    other_row = jnp.where(first, row_b, row_a)
    half_copy = pltpu.make_async_copy(lat_hbm.at[half_row], half_ref, sems.at[0])
    other_copy = pltpu.make_async_copy(lat_hbm.at[other_row], other_ref, sems.at[1])
    other_copy.start()
    half_copy.start()
    info_ref[0] = jnp.where(first, hop_b, hop_a) - 1
    info_ref[1] = half_row
    info_ref[2] = other_row
    other_copy.wait()
    half_copy.wait()


def picked(n, moves, latent):
    slot = jax.ShapeDtypeStruct(latent.shape[1:], latent.dtype)
    vmem = pl.BlockSpec(memory_space=pltpu.VMEM)
    smem = pl.BlockSpec(memory_space=pltpu.SMEM)
    return pl.pallas_call(
        functools.partial(pick, n),
        name="pick",
        out_shape=(slot, slot, jax.ShapeDtypeStruct((3,), jnp.int32)),
        in_specs=[smem, pl.BlockSpec(memory_space=pl.ANY)],
        out_specs=(vmem, vmem, smem),
        scratch_shapes=[pltpu.SemaphoreType.DMA((2,))],
        compiler_params=pltpu.CompilerParams(vmem_limit_bytes=GRANT),
    )(moves, latent)


def settle(info_ref, lat_hbm, half_hbm, attn_hbm, mixed_hbm, load_hbm,
           cache_out, attn_out, mixed_out, load_out,
           kept, half_v, attn_v, mixed_v, load_v, sem_in, sem_out):
    rows = lat_hbm.shape[0]
    half_row, other_row = info_ref[1], info_ref[2]

    def stays(r):
        return jnp.logical_and(half_row != r, other_row != r)

    def fetch(r):
        return pltpu.make_async_copy(lat_hbm.at[r], kept.at[r], sem_in.at[r])

    def put(r):
        return pltpu.make_async_copy(kept.at[r], cache_out.at[r], sem_out.at[r])

    through = [
        (half_hbm, half_v, cache_out.at[half_row]),
        (attn_hbm, attn_v, attn_out),
        (mixed_hbm, mixed_v, mixed_out),
        (load_hbm, load_v, load_out),
    ]
    ins = [pltpu.make_async_copy(a, b, sem_in.at[rows + k]) for k, (a, b, _) in enumerate(through)]
    outs = [pltpu.make_async_copy(b, o, sem_out.at[rows + k]) for k, (_, b, o) in enumerate(through)]
    for copy in ins:
        copy.start()
    for r in range(rows):
        pl.when(stays(r))(lambda r=r: fetch(r).start())
    for arrive, leave in zip(ins, outs):
        arrive.wait()
        leave.start()
    for r in range(rows):
        @pl.when(stays(r))
        def _(r=r):
            fetch(r).wait()
            put(r).start()
    for r in range(rows):
        pl.when(stays(r))(lambda r=r: put(r).wait())
    for copy in outs:
        copy.wait()


def settled(info, latent, half, attn, mixed, load):
    rows = latent.shape[0]
    hbm = pl.BlockSpec(memory_space=pl.ANY)

    def like(a):
        return jax.ShapeDtypeStruct(a.shape, a.dtype)

    def held(a):
        return pltpu.VMEM(a.shape, a.dtype)

    return pl.pallas_call(
        settle,
        name="settle",
        out_shape=(like(latent), like(attn), like(mixed), like(load)),
        in_specs=[pl.BlockSpec(memory_space=pltpu.SMEM)] + [hbm] * 5,
        out_specs=(hbm, hbm, hbm, hbm),
        scratch_shapes=[
            held(latent), held(half), held(attn), held(mixed), held(load),
            pltpu.SemaphoreType.DMA((rows + 4,)), pltpu.SemaphoreType.DMA((rows + 4,)),
        ],
        compiler_params=pltpu.CompilerParams(vmem_limit_bytes=GRANT),
        cost_estimate=pl.CostEstimate(flops=0, bytes_accessed=4 << 20, transcendentals=0),
    )(info, latent, half, attn, mixed, load)


def place(info_ref, other_ref, cache_in, cache_out, sem):
    copy = pltpu.make_async_copy(other_ref, cache_out.at[info_ref[2]], sem.at[0])
    copy.start()
    copy.wait()


def placed(info, other, cache):
    hbm = pl.BlockSpec(memory_space=pl.ANY)
    return pl.pallas_call(
        place,
        name="place",
        out_shape=jax.ShapeDtypeStruct(cache.shape, cache.dtype),
        in_specs=[pl.BlockSpec(memory_space=pltpu.SMEM), pl.BlockSpec(memory_space=pltpu.VMEM), hbm],
        out_specs=hbm,
        scratch_shapes=[pltpu.SemaphoreType.DMA((1,))],
        input_output_aliases={2: 0},
        compiler_params=pltpu.CompilerParams(vmem_limit_bytes=GRANT),
    )(info, other, cache)


def closing(steps, payload, info, latent, half, attn, mixed, load):
    arrival = shifted(payload, steps)
    cache, attn, mixed, load = settled(info, latent, half, attn, mixed, load)
    return placed(info, arrival, cache), attn, mixed, load


def shifted(value, steps):
    count = lax.axis_size("dev")
    pairs = [(source, (source + steps) % count) for source in range(count)]
    return lax.ppermute(value, "dev", pairs)


def per_device(
    q_lat, latent_cache, lengths, moves, hidden_in, norm_gain, w_up, w_down, queue_counts, deadline
):
    devices = lax.axis_size("dev")
    latent = jnp.swapaxes(latent_cache, 1, 2)
    half_payload, other_payload, info = picked(devices, moves.T, latent)
    attn, half_arrival, mixed, load = fused(
        devices, q_lat, latent, lengths, hidden_in, norm_gain, w_up, w_down,
        queue_counts, deadline, half_payload)
    branches = [functools.partial(closing, o) for o in range(1, devices)]
    new_cache, attn_out, mixed_out, load_out = lax.switch(
        info[0], branches, other_payload, info, latent, half_arrival, attn, mixed, load)
    return (attn_out, jnp.swapaxes(new_cache, 1, 2), mixed_out, load_out[0])


def solution(mesh):
    return jax.shard_map(
        per_device,
        mesh=mesh,
        in_specs=(
            P(("grp", "dev"), None, None),
            P(("grp", "dev"), None, None),
            P("grp"),
            P("grp", None),
            P(("grp", "dev"), None),
            P(),
            P(None, "dev"),
            P("dev", None),
            P(("grp", "dev"), None),
            P(("grp", "dev")),
        ),
        out_specs=(
            P(("grp", "dev"), None, None),
            P(("grp", "dev"), None, None),
            P(("grp", "dev"), None),
            P("grp"),
        ),
        check_vma=False,
    )
```

```python
import functools

import jax
import jax.numpy as jnp
from jax import lax
from jax.experimental import pallas as pl
from jax.experimental.pallas import tpu as pltpu
from jax.sharding import PartitionSpec as P

VL = 512
MOVE_DEV = 2
BUCKETS = 8
CORES = 2
GRANT = 67043328
MESH = pl.DeviceIdType.MESH

softmax_scale = 192.0 ** (-0.5)


def body(
    n,
    q_hbm, cache_hbm, len_ref, hid_ref, gain_ref, wu_hbm, wd_hbm, qc_ref, dl_ref, pay_hbm,
    attn_ref, arr_hbm, mixed_ref, load_ref,
    q_v, cache_v, wu_v, wd_v, allr, xs, x_v, hidden_v, part, rx1, red, rx2, loads,
    sem_in, sem_wu, sem_wd, ag_s, ag_r, fw_s, pay_s, pay_r, s1, r1, s2, r2, l_s, l_r,
):
    me = lax.axis_index("dev")
    chips = n // CORES
    z, c = me // CORES, me % CORES
    partner = z * CORES + (1 - c)
    rows, dim = hid_ref.shape
    nu, nd = wu_v.shape[0], wd_v.shape[0]
    cu, cd = wu_v.shape[2], wd_v.shape[2]
    half_rows = chips * rows

    def remote(src, dst, ss, rs, dev):
        return pltpu.make_async_remote_copy(
            src_ref=src, dst_ref=dst, send_sem=ss, recv_sem=rs,
            device_id={"dev": dev}, device_id_type=MESH)

    def up_copy(i):
        return pltpu.make_async_copy(
            wu_hbm.at[:, pl.ds(pl.multiple_of(i * cu, 128), cu)], wu_v.at[i], sem_wu.at[i])

    def down_copy(i):
        return pltpu.make_async_copy(
            wd_hbm.at[:, pl.ds(pl.multiple_of(i * cd, 128), cd)], wd_v.at[i], sem_wd.at[i])

    barrier = pltpu.get_barrier_semaphore()
    for o in range(1, n):
        pl.semaphore_signal(barrier, inc=1, device_id={"dev": lax.rem(me + o, n)},
                            device_id_type=MESH)
    q_copy = pltpu.make_async_copy(q_hbm, q_v, sem_in.at[0])
    cache_copy = pltpu.make_async_copy(cache_hbm, cache_v, sem_in.at[1])
    q_copy.start()
    cache_copy.start()
    for i in range(nu):
        up_copy(i).start()
    for i in range(nd):
        down_copy(i).start()

    widened = hid_ref[...].astype(jnp.float32)
    scaled = lax.rsqrt(jnp.mean(widened * widened, axis=-1, keepdims=True) + 1e-06)
    normed = widened * scaled * gain_ref[...].astype(jnp.float32).reshape(1, dim)
    allr[me] = normed.astype(jnp.bfloat16)
    buckets = lax.broadcasted_iota(jnp.int32, (1, BUCKETS), 1)
    counted = qc_ref[...].astype(jnp.float32)
    for r in range(rows):
        counted = counted + jnp.where(buckets == dl_ref[r], 1.0, 0.0)
    loads[me] = jnp.zeros((1, 128), jnp.float32)
    loads[me, :, 0:BUCKETS] = counted
    pl.semaphore_wait(barrier, n - 1)

    def gathered(src, ss, dev):
        return remote(allr.at[src], allr.at[src], ss, ag_r.at[src], dev)

    direct = [gathered(me, ag_s.at[0], partner)]
    for o in range(1, chips):
        direct.append(gathered(me, ag_s.at[o], lax.rem(z + o, chips) * CORES + c))
    for copy in direct[1:] + direct[:1]:
        copy.start()
    load_copies = []
    for o in range(1, n):
        copy = remote(loads.at[me], loads.at[me], l_s.at[o], l_r.at[me], lax.rem(me + o, n))
        copy.start()
        load_copies.append(copy)
    payload = remote(pay_hbm, arr_hbm, pay_s.at[0], pay_r.at[0], lax.rem(me + n // 2, n))
    payload.start()

    q_copy.wait()
    cache_copy.wait()

    def attend(r):
        latent = cache_v[r]
        scores = jnp.dot(q_v[r], latent, preferred_element_type=jnp.float32) * softmax_scale
        slots = lax.broadcasted_iota(jnp.int32, scores.shape, 1)
        included = slots < len_ref[me * rows + r]
        scores = jnp.where(included, scores, jnp.float32(-1e30))
        top = jnp.max(scores, axis=-1, keepdims=True)
        weights = jnp.where(included, jnp.exp(scores - top), jnp.float32(0.0))
        total = jnp.sum(weights, axis=-1, keepdims=True)
        summed = lax.dot_general(weights.astype(jnp.bfloat16), latent[:VL, :],
                                 (((1,), (1,)), ((), ())), preferred_element_type=jnp.float32)
        attn_ref[r] = (summed / total).astype(jnp.bfloat16)

    for r in range(rows // 2):
        attend(r)

    forwards = []
    for o in range(1, chips):
        src = lax.rem(z + chips - o, chips) * CORES + c
        gathered(src, ag_s.at[o], partner).wait_recv()
        copy = gathered(src, fw_s.at[o], partner)
        copy.start()
        forwards.append(copy)
    gathered(partner, ag_s.at[0], partner).wait_recv()
    for o in range(1, chips):
        src = lax.rem(z + chips - o, chips) * CORES + (1 - c)
        gathered(src, fw_s.at[o], partner).wait_recv()

    for d in range(n):
        at = ((d % CORES) * chips + d // CORES) * rows
        xs[at:at + rows, :] = allr[d].astype(jnp.float32)
    x_v[...] = xs[...].astype(jnp.bfloat16)

    def up_step(i, carry):
        up_copy(i).wait()
        up = jnp.dot(x_v[...], wu_v[i], preferred_element_type=jnp.float32)
        hidden_v[i] = (up / (1.0 + jnp.exp(-up))).astype(jnp.bfloat16)
        return carry

    lax.fori_loop(0, nu, up_step, 0)

    def swap(i):
        return remote(part.at[1 - c, i], rx1.at[i], s1.at[i], r1.at[i], partner)

    def scatter(i, o):
        to = lax.rem(z + o, chips)
        return remote(red.at[i, to], rx2.at[i, z], s2.at[i, o], r2.at[i, z], to * CORES + c)

    def reduce_step(i):
        swap(i).wait_recv()
        both = part[c, i] + rx1[i]
        for t in range(chips):
            red[i, t] = both[t * rows:(t + 1) * rows, :]
        for o in range(1, chips):
            scatter(i, o).start()

    def down_step(i, carry):
        down_copy(i).wait()
        acc = jnp.zeros((n * rows, cd), jnp.float32)
        for k in range(nu):
            acc = acc + jnp.dot(hidden_v[k], wd_v[i, k * cu:(k + 1) * cu, :],
                                preferred_element_type=jnp.float32)
        part[0, i] = acc[:half_rows]
        part[1, i] = acc[half_rows:]
        swap(i).start()

        @pl.when(i > 0)
        def _():
            reduce_step(i - 1)

        return carry

    lax.fori_loop(0, nd, down_step, 0)
    reduce_step(nd - 1)

    for r in range(rows // 2, rows):
        attend(r)

    for o in range(1, n):
        src = lax.rem(me + o, n)
        remote(loads.at[src], loads.at[src], l_s.at[o], l_r.at[src], src).wait_recv()
    total_load = loads[0]
    for d in range(1, n):
        total_load = total_load + loads[d]
    load_ref[...] = total_load[:, 0:BUCKETS]

    def finish(i, carry):
        acc = red[i, z]
        for o in range(1, chips):
            src = lax.rem(z + o, chips)
            remote(red.at[i, src], rx2.at[i, src], s2.at[i, o], r2.at[i, src],
                   src * CORES + c).wait_recv()
            acc = acc + rx2[i, src]
        cols = pl.ds(pl.multiple_of(i * cd, 128), cd)
        mixed_ref[:, cols] = (hid_ref[:, cols].astype(jnp.float32) + acc).astype(jnp.bfloat16)
        return carry

    lax.fori_loop(0, nd, finish, 0)

    def drain(i, carry):
        swap(i).wait_send()
        for o in range(1, chips):
            scatter(i, o).wait_send()
        return carry

    lax.fori_loop(0, nd, drain, 0)
    for copy in direct + forwards + load_copies:
        copy.wait_send()
    payload.wait()


def chunk_of(size, most):
    return max(w for w in range(128, most + 1, 128) if size % w == 0)


def fused(n, q_lat, latent_cache, lengths, hidden_in, gain, w_up, w_down, counts, deadline, payload):
    rows, dim = hidden_in.shape
    units = w_up.shape[1]
    heads, width = q_lat.shape[1:]
    context = latent_cache.shape[2]
    chips = n // CORES
    cu, cd = chunk_of(units, 256), chunk_of(dim, 512)
    nu, nd = units // cu, dim // cd
    bf, f32 = jnp.bfloat16, jnp.float32
    vmem, smem = pltpu.VMEM, pltpu.SMEM
    dma = pltpu.SemaphoreType.DMA

    def spec(space):
        return pl.BlockSpec(memory_space=space)

    return pl.pallas_call(
        functools.partial(body, n),
        name="fused",
        out_shape=(
            jax.ShapeDtypeStruct((rows, heads, VL), bf),
            jax.ShapeDtypeStruct((width, context), bf),
            jax.ShapeDtypeStruct((rows, dim), bf),
            jax.ShapeDtypeStruct((1, BUCKETS), f32),
        ),
        in_specs=[spec(pl.ANY), spec(pl.ANY), spec(smem), spec(vmem), spec(vmem), spec(pl.ANY),
                  spec(pl.ANY), spec(vmem), spec(smem), spec(pl.ANY)],
        out_specs=(spec(vmem), spec(pl.ANY), spec(vmem), spec(vmem)),
        scratch_shapes=[
            vmem((rows, heads, width), bf),
            vmem((rows, width, context), bf),
            vmem((nu, dim, cu), bf),
            vmem((nd, units, cd), bf),
            vmem((n, rows, dim), bf),
            vmem((n * rows, dim), f32),
            vmem((n * rows, dim), bf),
            vmem((nu, n * rows, cu), bf),
            vmem((CORES, nd, chips * rows, cd), f32),
            vmem((nd, chips * rows, cd), f32),
            vmem((nd, chips, rows, cd), f32),
            vmem((nd, chips, rows, cd), f32),
            vmem((n, 1, 128), f32),
            dma((2,)), dma((nu,)), dma((nd,)),
            dma((chips,)), dma((n,)), dma((chips,)),
            dma((1,)), dma((1,)),
            dma((nd,)), dma((nd,)), dma((nd, chips)), dma((nd, chips)),
            dma((n,)), dma((n,)),
        ],
        compiler_params=pltpu.CompilerParams(
            collective_id=0, has_side_effects=True, vmem_limit_bytes=GRANT),
    )(q_lat, latent_cache, lengths, hidden_in, gain, w_up, w_down, counts, deadline, payload)


def pick(n, moves_ref, lat_hbm, half_ref, other_ref, info_ref, sems):
    me = lax.axis_index("dev")
    rows = lat_hbm.shape[0]
    row_a = moves_ref[0, me] - me * rows
    row_b = moves_ref[0, n + me] - me * rows
    hop_a = lax.rem(moves_ref[2, me] - me + n, n)
    hop_b = lax.rem(moves_ref[2, n + me] - me + n, n)
    first = hop_a == n // 2
    half_row = jnp.where(first, row_a, row_b)
    other_row = jnp.where(first, row_b, row_a)
    half_copy = pltpu.make_async_copy(lat_hbm.at[half_row], half_ref, sems.at[0])
    other_copy = pltpu.make_async_copy(lat_hbm.at[other_row], other_ref, sems.at[1])
    other_copy.start()
    half_copy.start()
    info_ref[0] = jnp.where(first, hop_b, hop_a) - 1
    info_ref[1] = half_row
    info_ref[2] = other_row
    other_copy.wait()
    half_copy.wait()


def picked(n, moves, latent):
    slot = jax.ShapeDtypeStruct(latent.shape[1:], latent.dtype)
    vmem = pl.BlockSpec(memory_space=pltpu.VMEM)
    smem = pl.BlockSpec(memory_space=pltpu.SMEM)
    return pl.pallas_call(
        functools.partial(pick, n),
        name="pick",
        out_shape=(slot, slot, jax.ShapeDtypeStruct((3,), jnp.int32)),
        in_specs=[smem, pl.BlockSpec(memory_space=pl.ANY)],
        out_specs=(vmem, vmem, smem),
        scratch_shapes=[pltpu.SemaphoreType.DMA((2,))],
        compiler_params=pltpu.CompilerParams(vmem_limit_bytes=GRANT),
    )(moves, latent)


def settle(info_ref, lat_hbm, half_hbm, attn_hbm, mixed_hbm, load_hbm,
           cache_out, attn_out, mixed_out, load_out,
           kept, half_v, attn_v, mixed_v, load_v, sem_in, sem_out):
    rows = lat_hbm.shape[0]
    half_row, other_row = info_ref[1], info_ref[2]

    def stays(r):
        return jnp.logical_and(half_row != r, other_row != r)

    def fetch(r):
        return pltpu.make_async_copy(lat_hbm.at[r], kept.at[r], sem_in.at[r])

    def put(r):
        return pltpu.make_async_copy(kept.at[r], cache_out.at[r], sem_out.at[r])

    through = [
        (half_hbm, half_v, cache_out.at[half_row]),
        (attn_hbm, attn_v, attn_out),
        (mixed_hbm, mixed_v, mixed_out),
        (load_hbm, load_v, load_out),
    ]
    ins = [pltpu.make_async_copy(a, b, sem_in.at[rows + k]) for k, (a, b, _) in enumerate(through)]
    outs = [pltpu.make_async_copy(b, o, sem_out.at[rows + k]) for k, (_, b, o) in enumerate(through)]
    for copy in ins:
        copy.start()
    for r in range(rows):
        pl.when(stays(r))(lambda r=r: fetch(r).start())
    for arrive, leave in zip(ins, outs):
        arrive.wait()
        leave.start()
    for r in range(rows):
        @pl.when(stays(r))
        def _(r=r):
            fetch(r).wait()
            put(r).start()
    for r in range(rows):
        pl.when(stays(r))(lambda r=r: put(r).wait())
    for copy in outs:
        copy.wait()


def settled(info, latent, half, attn, mixed, load):
    rows = latent.shape[0]
    hbm = pl.BlockSpec(memory_space=pl.ANY)

    def like(a):
        return jax.ShapeDtypeStruct(a.shape, a.dtype)

    def held(a):
        return pltpu.VMEM(a.shape, a.dtype)

    return pl.pallas_call(
        settle,
        name="settle",
        out_shape=(like(latent), like(attn), like(mixed), like(load)),
        in_specs=[pl.BlockSpec(memory_space=pltpu.SMEM)] + [hbm] * 5,
        out_specs=(hbm, hbm, hbm, hbm),
        scratch_shapes=[
            held(latent), held(half), held(attn), held(mixed), held(load),
            pltpu.SemaphoreType.DMA((rows + 4,)), pltpu.SemaphoreType.DMA((rows + 4,)),
        ],
        compiler_params=pltpu.CompilerParams(vmem_limit_bytes=GRANT),
        cost_estimate=pl.CostEstimate(flops=0, bytes_accessed=4 << 20, transcendentals=0),
    )(info, latent, half, attn, mixed, load)


def place(info_ref, other_ref, cache_in, cache_out, sem):
    copy = pltpu.make_async_copy(other_ref, cache_out.at[info_ref[2]], sem.at[0])
    copy.start()
    copy.wait()


def placed(info, other, cache):
    hbm = pl.BlockSpec(memory_space=pl.ANY)
    return pl.pallas_call(
        place,
        name="place",
        out_shape=jax.ShapeDtypeStruct(cache.shape, cache.dtype),
        in_specs=[pl.BlockSpec(memory_space=pltpu.SMEM), pl.BlockSpec(memory_space=pltpu.VMEM), hbm],
        out_specs=hbm,
        scratch_shapes=[pltpu.SemaphoreType.DMA((1,))],
        input_output_aliases={2: 0},
        compiler_params=pltpu.CompilerParams(vmem_limit_bytes=GRANT),
    )(info, other, cache)


def closing(steps, payload, info, latent, half, attn, mixed, load):
    arrival = shifted(payload, steps)
    cache, attn, mixed, load = settled(info, latent, half, attn, mixed, load)
    return placed(info, arrival, cache), attn, mixed, load


def shifted(value, steps):
    count = lax.axis_size("dev")
    pairs = [(source, (source + steps) % count) for source in range(count)]
    return lax.ppermute(value, "dev", pairs)


def per_device(
    q_lat, latent_cache, lengths, moves, hidden_in, norm_gain, w_up, w_down, queue_counts, deadline
):
    devices = lax.axis_size("dev")
    latent = jnp.swapaxes(latent_cache, 1, 2)
    half_payload, other_payload, info = picked(devices, moves.T, latent)
    attn, half_arrival, mixed, load = fused(
        devices, q_lat, latent, lengths, hidden_in, norm_gain, w_up, w_down,
        queue_counts, deadline, half_payload)
    branches = [functools.partial(closing, o) for o in range(1, devices)]
    new_cache, attn_out, mixed_out, load_out = lax.switch(
        info[0], branches, other_payload, info, latent, half_arrival, attn, mixed, load)
    return (attn_out, jnp.swapaxes(new_cache, 1, 2), mixed_out, load_out[0])


def solution(mesh):
    return jax.shard_map(
        per_device,
        mesh=mesh,
        in_specs=(
            P(("grp", "dev"), None, None),
            P(("grp", "dev"), None, None),
            P("grp"),
            P("grp", None),
            P(("grp", "dev"), None),
            P(),
            P(None, "dev"),
            P("dev", None),
            P(("grp", "dev"), None),
            P(("grp", "dev")),
        ),
        out_specs=(
            P(("grp", "dev"), None, None),
            P(("grp", "dev"), None, None),
            P(("grp", "dev"), None),
            P("grp"),
        ),
        check_vma=False,
    )
```
